32 devices in a mesh: grp: 8 (over z, core), dev: 4 (over y, x).
Axes of the slice: x: 2, y: 2, z: 4, core: 2. Of those that a mesh axis runs over, the one named last changes fastest.
Arguments:
- query_hidden: bfloat16 [32, 32, 3584], P(('grp', 'dev')), may hold values from -6 to 6
- projection: bfloat16 [3584, 128], replicated, may hold values from -0.09375 to 0.09375
- page_embed: bfloat16 [32, 1024, 128], P('grp', 'dev'), may hold values from -6 to 6
- page_counts: int32 [32], replicated, may hold values from 128 to 1024, as said below
- positive: int32 [32], replicated, may hold values from 0 to 31
- hard_negs: int32 [32, 2], replicated, may hold values from 0 to 31
- loss_weight: float32 [32], replicated, may hold values from 0.5 to 2
Outputs:
- losses: float32 [32], P(('grp', 'dev'))
- hidden_grad: bfloat16 [32, 32, 3584], P(('grp', 'dev'))
- proj_grad: float32 [3584, 128], P(('grp', 'dev'))
- pages_grad: bfloat16 [32, 1024, 128], P('grp', 'dev')
The draws below stay inside these ranges and needn't reach their ends.
Inputs may be any that keep to these rules, and one draw needn't show every extreme that they name: The first page_counts[p] tokens of page p are valid; some page has all 1024 tokens valid. `hard_negs`: a hard negative may repeat or equal the positive page.
All inputs are finite; a program needn't handle non-finite values.
Results may differ from the reference program's by a relative error of at most 0.018.
Values may be sent and summed in bfloat16 or wider, within the bound.
A program may use at most 64 MiB of HBM per device.

```python
import math
import jax
import jax.numpy as jnp
from jax import lax

H = 3584
DIM = 128
QT = 32
PT = 1024
NHN = 2
Q = 32
P_SIZE = 32


def draw_page_counts(key, part):
    count_key, pick_key = jax.random.split(jax.random.fold_in(key, 11))
    counts = jax.random.randint(count_key, (P_SIZE,), PT // 8, PT + 1)
    full_page = jax.random.randint(pick_key, (), 0, P_SIZE)
    return jnp.where(jnp.arange(P_SIZE) == full_page, PT, counts).astype(jnp.int32)


def plant(values, rng, low, largest):
    longest = values.shape.index(max(values.shape))
    spots = []
    for shift in (0, 1):
        where = [jax.random.randint(jax.random.fold_in(rng, axis), (), 0, length) for axis, length in enumerate(values.shape)]
        where[longest] = (where[longest] + shift) % values.shape[longest]
        spots.append(tuple(where))
    return values.at[spots[0]].set(low).at[spots[1]].set(largest)


def levels(key, dims, cuts, least, high):
    loudness, own = 1.0, jax.random.fold_in(key, 6)
    for axis_at, shards_of in cuts:
        draws = jnp.exp(jax.random.uniform(jax.random.fold_in(own, axis_at), (shards_of,), jnp.float32, least / len(cuts), high / len(cuts)))
        loudness = loudness * jnp.repeat(draws, dims[axis_at] // shards_of).reshape([-1 if axis == axis_at else 1 for axis in range(len(dims))])
    return loudness


def noise(key, shape, scale, bound, cuts=(), kind=jnp.bfloat16):
    result = jax.random.normal(key, shape, jnp.float32) * scale
    if len(cuts) > 0:
        result = levels(key, shape, cuts, -0.22, 0.18) * result
    return jnp.clip(result, min=-bound, max=bound).astype(kind)


def setup_inputs(seed: int = 0) -> dict:
    arg_keys = jax.random.split(jax.random.key(seed), 8)
    return {
        "query_hidden": noise(arg_keys[0], (Q, QT, H), 1.0, 6.0, ((0, 32),)),
        "projection": noise(arg_keys[1], (H, DIM), H ** -0.5, 0.09375),
        "page_embed": noise(arg_keys[2], (P_SIZE, PT, DIM), 1.0, 6.0, ((0, 8), (1, 4))),
        "page_counts": draw_page_counts(jax.random.fold_in(arg_keys[7], 71), 0),
        "positive": plant(jax.random.randint(arg_keys[4], (Q,), 0, P_SIZE), jax.random.fold_in(arg_keys[4], 1), 0, P_SIZE - 1).astype(jnp.int32),
        "hard_negs": plant(jax.random.randint(arg_keys[5], (Q, NHN), 0, P_SIZE), jax.random.fold_in(arg_keys[5], 1), 0, P_SIZE - 1).astype(jnp.int32),
        "loss_weight": jnp.clip(jax.random.uniform(arg_keys[6], (Q,), jnp.float32, 0.5, 2.0), 0.5, 2.0),
    }


SOFTMAX_HEAT = 0.02
EPSILON = 1e-06

def unit_rows(values):
    row_scale = lax.rsqrt(lax.optimization_barrier(jnp.sum(values * values, axis=-1, keepdims=True)) + EPSILON)
    return (values * row_scale, row_scale)

def unit_back(unit_vec, row_scale, gradient):
    projected = lax.optimization_barrier(jnp.sum(unit_vec * gradient, axis=-1, keepdims=True))
    return (gradient - unit_vec * projected) * row_scale

def token_sums(queries, page_vecs, page_live, row_tile, page_tile):
    query_matrix = queries.shape[0]
    embed_width = queries.shape[1]
    total_pages = page_vecs.shape[0]
    slice_length = page_vecs.shape[1]
    row_steps = query_matrix // row_tile
    page_steps = total_pages // page_tile
    query_blocks = queries.reshape(row_steps, row_tile, embed_width)
    vec_blocks = page_vecs.reshape(page_steps, page_tile * slice_length, embed_width)
    live_blocks = page_live.reshape(page_steps, page_tile * slice_length)

    def per_rows(query_part):

        def per_pages(inputs):
            vec_part, active_share = inputs
            score_matrix = lax.dot_general(query_part, vec_part, (((1,), (1,)), ((), ())), preferred_element_type=jnp.float32)
            weight_vector = jnp.exp(score_matrix / SOFTMAX_HEAT) * active_share[None, :]
            return lax.optimization_barrier(jnp.sum(weight_vector.reshape(row_tile, page_tile, slice_length), axis=2))
        return lax.map(per_pages, (vec_blocks, live_blocks))
    partial_value = lax.map(per_rows, query_blocks)
    return partial_value.transpose(0, 2, 1, 3).reshape(query_matrix, total_pages)

def backward_pass(queries, page_vecs, page_live, row_scales, row_tile, page_tile):
    query_matrix = queries.shape[0]
    embed_width = queries.shape[1]
    total_pages = page_vecs.shape[0]
    slice_length = page_vecs.shape[1]
    row_steps = query_matrix // row_tile
    page_steps = total_pages // page_tile
    query_blocks = queries.reshape(row_steps, row_tile, embed_width)
    vec_blocks = page_vecs.reshape(page_steps, page_tile * slice_length, embed_width)
    live_blocks = page_live.reshape(page_steps, page_tile * slice_length)
    scale_blocks = row_scales.reshape(row_steps, row_tile, page_steps, page_tile).transpose(0, 2, 1, 3)

    def per_rows(vec_grads, inputs):
        query_part, scale_part = inputs

        def per_pages(inner_in):
            vec_part, active_share, factor = inner_in
            score_matrix = lax.dot_general(query_part, vec_part, (((1,), (1,)), ((), ())), preferred_element_type=jnp.float32)
            weight_vector = (jnp.exp(score_matrix / SOFTMAX_HEAT) * active_share[None, :]).reshape(row_tile, page_tile, slice_length)
            weight_vector = (weight_vector * factor[:, :, None]).reshape(row_tile, page_tile * slice_length).astype(jnp.bfloat16)
            query_grad = jnp.dot(weight_vector, vec_part, preferred_element_type=jnp.float32)
            vec_grad = lax.dot_general(weight_vector, query_part, (((0,), (0,)), ((), ())), preferred_element_type=jnp.float32)
            return (query_grad, vec_grad)
        query_grads, new_grads = lax.map(per_pages, (vec_blocks, live_blocks, scale_part))
        return (vec_grads + new_grads, lax.optimization_barrier(jnp.sum(query_grads, axis=0)))
    start_grads = jnp.zeros((page_steps, page_tile * slice_length, embed_width), jnp.float32)
    vec_grads, query_grads = lax.scan(per_rows, start_grads, (query_blocks, scale_blocks))
    return (query_grads.reshape(query_matrix, embed_width), vec_grads.reshape(total_pages, slice_length, embed_width))

def score_table(totals, query_length, count_values):
    query_matrix = totals.shape[0]
    total_pages = totals.shape[1]
    average_values = totals / count_values[None, :]
    return lax.optimization_barrier(jnp.sum((SOFTMAX_HEAT * jnp.log(average_values)).reshape(query_matrix // query_length, query_length, total_pages), axis=1))

def page_hits(positive, hard_negs, page_ids):
    pos_hot = (positive[:, None] == page_ids[None, :]).astype(jnp.float32)
    neg_hot = (hard_negs[:, :, None] == page_ids[None, None, :]).astype(jnp.float32)
    return (pos_hot, neg_hot)

def query_terms(exp_sum, pos_score, neg_score):
    log_total = jnp.log(exp_sum)
    margin = neg_score - pos_score[:, None]
    losses = log_total - pos_score + lax.optimization_barrier(jnp.mean(jax.nn.softplus(margin), axis=1))
    return (losses, log_total, jax.nn.sigmoid(margin))

def score_grads(score_matrix, log_total, pull_terms, pos_hot, neg_hot, weight_vector):
    neg_count = neg_hot.shape[1]
    push_terms = lax.optimization_barrier(jnp.sum(pull_terms[:, :, None] * (neg_hot - pos_hot[:, None, :]), axis=1)) / neg_count
    return weight_vector[:, None] * (jnp.exp(score_matrix - log_total[:, None]) - pos_hot + push_terms)

def expand_rows(score_grad, totals, query_length):
    query_matrix = totals.shape[0]
    total_pages = totals.shape[1]
    shaped = totals.reshape(query_matrix // query_length, query_length, total_pages)
    return (score_grad[:, None, :] / shaped).reshape(query_matrix, total_pages)

def reference(query_hidden, projection, page_embed, page_counts, positive, hard_negs, loss_weight):
    query_count, query_length, hidden_width = query_hidden.shape
    total_pages, page_len, embed_width = page_embed.shape
    hidden_rows = query_hidden.reshape(query_count * query_length, hidden_width)
    query_raw = jnp.dot(hidden_rows, projection, preferred_element_type=jnp.float32)
    query_unit, query_scale = unit_rows(query_raw)
    query_norm = query_unit.astype(jnp.bfloat16)
    page_unit, page_scale = unit_rows(page_embed.astype(jnp.float32))
    page_norm = page_unit.astype(jnp.bfloat16)
    positions = jnp.arange(page_len).astype(jnp.int32)
    page_live = (positions[None, :] < page_counts[:, None]).astype(jnp.float32)
    count_values = page_counts.astype(jnp.float32)
    row_tile = math.gcd(query_count * query_length, 512)
    page_tile = math.gcd(total_pages, max(1, 1024 // page_len))
    totals = token_sums(query_norm, page_norm, page_live, row_tile, page_tile)
    score_matrix = score_table(totals, query_length, count_values)
    page_ids = jnp.arange(total_pages).astype(jnp.int32)
    pos_hot, neg_hot = page_hits(positive, hard_negs, page_ids)
    exp_sum = lax.optimization_barrier(jnp.sum(jnp.exp(score_matrix), axis=1))
    pos_score = lax.optimization_barrier(jnp.sum(score_matrix * pos_hot, axis=1))
    neg_score = lax.optimization_barrier(jnp.sum(score_matrix[:, None, :] * neg_hot, axis=2))
    losses, log_total, pull_terms = query_terms(exp_sum, pos_score, neg_score)
    score_grad = score_grads(score_matrix, log_total, pull_terms, pos_hot, neg_hot, loss_weight)
    row_scales = expand_rows(score_grad, totals, query_length)
    query_grad, page_grad = backward_pass(query_norm, page_norm, page_live, row_scales, row_tile, page_tile)
    raw_grad = unit_back(query_unit, query_scale, query_grad).astype(jnp.bfloat16)
    hidden_grad = lax.dot_general(raw_grad, projection, (((1,), (1,)), ((), ())), preferred_element_type=jnp.float32)
    hidden_grad = hidden_grad.astype(jnp.bfloat16).reshape(query_count, query_length, hidden_width)
    proj_grad = lax.dot_general(hidden_rows, raw_grad, (((0,), (0,)), ((), ())), preferred_element_type=jnp.float32)
    pages_grad = unit_back(page_unit, page_scale, page_grad).astype(jnp.bfloat16)
    return (losses, hidden_grad, proj_grad, pages_grad)
```

```python
import functools
import math

import jax
import jax.numpy as jnp
from jax import lax
from jax.experimental import pallas as pl
from jax.experimental.pallas import tpu as pltpu
from jax.sharding import PartitionSpec as P

SOFTMAX_HEAT = 0.02
EPSILON = 1e-06
MESH = pl.DeviceIdType.MESH
NT = (((1,), (1,)), ((), ()))
F32 = jnp.float32
BF16 = jnp.bfloat16


def split3(x):
    a = x.astype(BF16)
    r = x - a.astype(F32)
    b = r.astype(BF16)
    c = (r - b.astype(F32)).astype(BF16)
    return a, b, c


def dot3(x, ind):
    a, b, c = split3(x)
    return (
        jnp.dot(c, ind, preferred_element_type=F32)
        + jnp.dot(b, ind, preferred_element_type=F32)
        + jnp.dot(a, ind, preferred_element_type=F32)
    )


def kernel(
    groups, members, qlen, nhn, nb,
    hid_in, proj_in, page_in, counts_in, crow_in, pos_in, neg_in, lw_in,
    loss_ref, hgrad_ref, pgrad_ref, pagegrad_ref,
    qsend, qall, pn, pscale, pnt, ebuf, tot, tx, tall, totz, sgbuf, ind_down, ind_up, hsplit, hall, hallt, projt,
    wbuf, qg, rs, rg, rg_all, pgsend, pgrecv, psend, precv,
    send_sems, recv_sems, q_sems,
    hid_ref, proj_ref, page_ref, counts_ref, crow_ref, pos_ref, neg_ref, lw_ref, load_sems,
):
    loads = [
        pltpu.make_async_copy(src, dst, load_sems.at[i])
        for i, (src, dst) in enumerate(
            (
                (hid_in, hid_ref), (proj_in, proj_ref), (page_in, page_ref), (counts_in, counts_ref),
                (crow_in, crow_ref), (pos_in, pos_ref), (neg_in, neg_ref), (lw_in, lw_ref),
            )
        )
    ]
    for load in loads:
        load.start()

    n = groups * members
    pair = pn.shape[0]
    chips = n // pair
    zs = groups // pair
    rows, hidden = hid_ref.shape
    pages_here, slice_len, dim = page_ref.shape
    both = pair * pages_here
    n_chunks = chips // nb
    cq = nb * rows
    q_here = rows // qlen
    q_total = n * q_here
    hb = hidden // n
    hb_pad = hallt.shape[1]
    gi = lax.axis_index("grp")
    mi = lax.axis_index("dev")
    me = gi * members + mi
    core = lax.rem(gi, pair)
    zi = lax.div(gi, pair)
    chip = zi * members + mi
    my_chunk = lax.div(chip, nb)
    partner = (gi + 1 - 2 * core, mi)

    def place(dst):
        return (lax.div(dst, members) * pair + core, lax.rem(dst, members))

    barrier = pltpu.get_barrier_semaphore()

    def greet(k, carry):
        where = place(lax.rem(chip + k, chips))
        pl.semaphore_signal(barrier, inc=1, device_id=where, device_id_type=MESH)
        return carry

    lax.fori_loop(1, chips, greet, 0)
    if pair > 1:
        pl.semaphore_signal(barrier, inc=1, device_id=partner, device_id_type=MESH)

    def done(ref, sem):
        pltpu.make_async_copy(ref, ref, sem).wait()

    def to_plane(src, dst, send_sem, recv_sem):
        def send(k, carry):
            where = place(lax.rem(chip + k, chips))
            pltpu.make_async_remote_copy(
                src, dst, send_sem, recv_sem, device_id=where, device_id_type=MESH
            ).start()
            return carry

        lax.fori_loop(1, chips, send, 0)

    def to_partner(src, dst, i):
        pltpu.make_async_remote_copy(
            src, dst, send_sems.at[i], recv_sems.at[i], device_id=partner, device_id_type=MESH
        ).start()

    loads[0].wait()
    loads[1].wait()
    query_raw = jnp.dot(hid_ref[...], proj_ref[...], preferred_element_type=F32)
    query_scale = lax.rsqrt(jnp.sum(query_raw * query_raw, axis=-1, keepdims=True) + EPSILON)
    query_unit = query_raw * query_scale
    qsend[...] = query_unit.astype(BF16)

    pl.semaphore_wait(barrier, chips - 1 + pair - 1)

    pltpu.make_async_copy(qsend, qall.at[chip], q_sems.at[my_chunk]).start()
    to_plane(qsend, qall.at[chip], send_sems.at[0], q_sems.at[my_chunk])

    loads[2].wait()
    for p in range(pages_here):
        praw = page_ref[p].astype(F32)
        ps = lax.rsqrt(jnp.sum(praw * praw, axis=-1, keepdims=True) + EPSILON)
        pscale[p] = ps
        pn[core, p] = (praw * ps).astype(BF16)
    if pair > 1:
        to_partner(pn.at[core], pn.at[core], 6)

    for j in range(chips):
        zj, mj = divmod(j, members)
        for h in range(pair):
            d = (zj * pair + h) * members + mj
            hsplit[j, :, h * hb_pad : h * hb_pad + hb] = hid_ref[:, d * hb : (d + 1) * hb]
            if hb_pad > hb:
                hsplit[j, :, h * hb_pad + hb : (h + 1) * hb_pad] = jnp.zeros((rows, hb_pad - hb), BF16)
    pltpu.make_async_copy(hsplit.at[chip], hall.at[chip], recv_sems.at[3]).start()

    def send_h(k, carry):
        dst = lax.rem(chip + k, chips)
        pltpu.make_async_remote_copy(
            hsplit.at[dst], hall.at[chip], send_sems.at[3], recv_sems.at[3],
            device_id=place(dst), device_id_type=MESH,
        ).start()
        return carry

    lax.fori_loop(1, chips, send_h, 0)

    projt[...] = jnp.transpose(proj_ref[...])

    q_row = lax.broadcasted_iota(jnp.int32, (1, q_total), 1)
    q_col = lax.broadcasted_iota(jnp.int32, (q_total, 1), 0)

    def first_token(q):
        dev = lax.div(q, q_here)
        grp = lax.div(dev, members)
        at = (lax.div(grp, pair) * members + lax.rem(dev, members)) * rows + lax.rem(q, q_here) * qlen
        return jnp.where(lax.rem(grp, pair) == core, at, -qlen)

    row_start = first_token(q_row)
    col_start = first_token(q_col)

    def indicators(c, carry):
        r = lax.broadcasted_iota(jnp.int32, (cq, q_total), 0) + c * cq
        ind_down[c] = jnp.where((r >= row_start) & (r < row_start + qlen), 1.0, 0.0).astype(BF16)
        r = lax.broadcasted_iota(jnp.int32, (q_total, cq), 1) + c * cq
        ind_up[c] = jnp.where((r >= col_start) & (r < col_start + qlen), 1.0, 0.0).astype(BF16)
        return carry

    lax.fori_loop(0, n_chunks, indicators, 0)

    for load in loads[3:]:
        load.wait()
    token = lax.broadcasted_iota(jnp.int32, (slice_len, 1), 0) + mi * slice_len
    biases = []
    for p in range(both):
        count = counts_ref[zi * both + p]
        biases.append(jnp.where(token < count, 0.0, -1e30).astype(F32))

    page_total = groups * pages_here
    pos_row = pos_ref[...].astype(F32)
    neg_rows = [neg_ref[j : j + 1, :].astype(F32) for j in range(nhn)]
    lw_row = lw_ref[...]
    eye = lax.broadcasted_iota(jnp.int32, (page_total, page_total), 0) == lax.broadcasted_iota(
        jnp.int32, (page_total, page_total), 1
    )
    count_col = jnp.sum(jnp.where(eye, crow_ref[...].astype(F32), 0.0), axis=1, keepdims=True)
    log_count = (SOFTMAX_HEAT * qlen) * jnp.log(count_col)
    page_id = lax.broadcasted_iota(jnp.int32, (page_total, q_total), 0).astype(F32)
    pos_hot = jnp.where(page_id == pos_row, 1.0, 0.0)
    neg_hots = [jnp.where(page_id == row, 1.0, 0.0) for row in neg_rows]

    if pair > 1:
        done(pn.at[1 - core], recv_sems.at[6])

    def forward(i, carry):
        c = lax.rem(my_chunk + i, n_chunks)
        done(qall.at[pl.ds(0, nb)], q_sems.at[c])
        qc = qall[pl.ds(c * nb, nb)].reshape(cq, dim)
        parts = []
        for p in range(both):
            s = lax.dot_general(pn[p // pages_here, p % pages_here], qc, NT, preferred_element_type=F32)
            e = jnp.exp(s * (1.0 / SOFTMAX_HEAT) + biases[p])
            ebuf[c, p] = e
            parts.append(jnp.sum(e, axis=0, keepdims=True))
        tot[c] = jnp.concatenate(parts, axis=0)
        return carry

    lax.fori_loop(0, n_chunks, forward, 0)

    tx[...] = tot[...].reshape(n_chunks * both, cq).astype(BF16)
    pltpu.make_async_copy(tx, tall.at[chip], recv_sems.at[1]).start()
    to_plane(tx, tall.at[chip], send_sems.at[1], recv_sems.at[1])

    pnt[...] = jnp.transpose(pn[...].reshape(both * slice_len, dim))

    done(tall, recv_sems.at[1])

    for z in range(zs):

        def add_slices(m, acc):
            return acc + tall[z * members + m].astype(F32)

        if members <= 4:
            total = tall[z * members].astype(F32)
            for m in range(1, members):
                total = add_slices(m, total)
        else:
            total = lax.fori_loop(0, members, add_slices, jnp.zeros((n_chunks * both, cq), F32))
        totz[z] = total.reshape(n_chunks, both, cq)

    def compress(c, acc):
        return acc + dot3(jnp.log(totz[:, c].reshape(zs * both, cq)), ind_down[c])

    acc = jnp.zeros((page_total, q_total), F32)
    if n_chunks <= 4:
        for c in range(n_chunks):
            acc = compress(c, acc)
    else:
        acc = lax.fori_loop(0, n_chunks, compress, acc)
    scores = SOFTMAX_HEAT * acc - log_count

    log_total = jnp.log(jnp.sum(jnp.exp(scores), axis=0, keepdims=True))
    pos_score = jnp.sum(scores * pos_hot, axis=0, keepdims=True)
    soft = jnp.zeros((1, q_total), F32)
    push = jnp.zeros((page_total, q_total), F32)
    for j in range(nhn):
        margin = jnp.sum(scores * neg_hots[j], axis=0, keepdims=True) - pos_score
        small = jnp.exp(-jnp.abs(margin))
        soft = soft + jnp.maximum(margin, 0.0) + jnp.log1p(small)
        sig = jnp.where(margin >= 0, 1.0, small) / (1.0 + small)
        push = push + sig * (neg_hots[j] - pos_hot)
    losses = log_total - pos_score + soft / nhn
    grads = lw_row * (jnp.exp(scores - log_total) - pos_hot + push / nhn)
    for z in range(zs):
        sgbuf[z] = grads[z * both : (z + 1) * both, :]
    score_grad = sgbuf[zi]
    grad3 = split3(score_grad)

    def backward(i, carry):
        c = lax.rem(my_chunk + 1 + i, n_chunks)
        ind = ind_up[c]
        wide = (
            jnp.dot(grad3[2], ind, preferred_element_type=F32)
            + jnp.dot(grad3[1], ind, preferred_element_type=F32)
            + jnp.dot(grad3[0], ind, preferred_element_type=F32)
        )
        factor = wide / totz[zi, c]
        for p in range(both):
            wbuf[c, p] = (ebuf[c, p] * factor[p : p + 1, :]).astype(BF16)
        w = wbuf[c].reshape(both * slice_len, cq)
        gt = jnp.dot(pnt[...], w, preferred_element_type=F32)
        qg[pl.ds(c * nb, nb)] = jnp.transpose(gt).astype(BF16).reshape(nb, rows, dim)

        def send(k, carry2):
            dst = c * nb + k

            @pl.when(dst != chip)
            def _():
                pltpu.make_async_remote_copy(
                    qg.at[dst], rs.at[chip], send_sems.at[4], recv_sems.at[4],
                    device_id=place(dst), device_id_type=MESH,
                ).start()

            return carry2

        lax.fori_loop(0, nb, send, 0)
        return carry

    lax.fori_loop(0, n_chunks, backward, 0)
    pltpu.make_async_copy(qg.at[chip], rs.at[chip], recv_sems.at[4]).start()

    lane = lax.broadcasted_iota(jnp.int32, (1, q_total), 1)
    for i in range(q_here):
        loss_ref[i] = jnp.sum(jnp.where(lane == me * q_here + i, losses, 0.0))

    def page_grad(half, p):
        def page_step(c, acc):
            qc = qall[pl.ds(c * nb, nb)].reshape(cq, dim)
            return acc + jnp.dot(wbuf[c, half * pages_here + p], qc, preferred_element_type=F32)

        acc = jnp.zeros((slice_len, dim), F32)
        if n_chunks <= 4:
            for c in range(n_chunks):
                acc = page_step(c, acc)
            return acc
        return lax.fori_loop(0, n_chunks, page_step, acc)

    if pair > 1:
        for p in range(pages_here):
            pgsend[p] = page_grad(1 - core, p).astype(BF16)
        to_partner(pgsend, pgrecv, 7)

    done(hall, recv_sems.at[3])
    for h in range(pair):
        hallt[h] = jnp.transpose(hall[:, :, h * hb_pad : (h + 1) * hb_pad].reshape(chips * rows, hb_pad))

    own_grads = [page_grad(core, p) for p in range(pages_here)]
    if pair > 1:
        done(pgrecv, recv_sems.at[7])
    for p in range(pages_here):
        pg = own_grads[p]
        if pair > 1:
            pg = pg + pgrecv[p].astype(F32)
        ps = pscale[p]
        pu = page_ref[p].astype(F32) * ps
        back = jnp.sum(pu * pg, axis=-1, keepdims=True)
        pagegrad_ref[p] = ((pg - pu * back) * ps).astype(BF16)

    done(rs, recv_sems.at[4])
    sum_step = 8 if chips % 8 == 0 else 1

    def add(i, acc):
        return acc + jnp.sum(rs[pl.ds(i * sum_step, sum_step)].astype(F32), axis=0)

    query_grad = lax.fori_loop(0, chips // sum_step, add, jnp.zeros((rows, dim), F32))
    along = jnp.sum(query_unit * query_grad, axis=-1, keepdims=True)
    raw_grad = ((query_grad - query_unit * along) * query_scale).astype(BF16)
    rg[...] = raw_grad

    pltpu.make_async_copy(rg, rg_all.at[chip], recv_sems.at[5]).start()
    to_plane(rg, rg_all.at[chip], send_sems.at[5], recv_sems.at[5])

    hgrad_ref[...] = jnp.dot(raw_grad, projt[...], preferred_element_type=F32).astype(BF16)

    done(rg_all, recv_sems.at[5])
    rga = rg_all[...].reshape(chips * rows, dim)
    if pair > 1:
        psend[...] = jnp.dot(hallt[1 - core], rga, preferred_element_type=F32)
        to_partner(psend, precv, 8)
    pgrad = jnp.dot(hallt[core], rga, preferred_element_type=F32)
    if pair > 1:
        done(precv, recv_sems.at[8])
        pgrad = pgrad + precv[...]
    pgrad_ref[...] = pgrad[:hb]
    if chips > 1:
        done(qall.at[pl.ds(0, chips - 1)], send_sems.at[0])
        done(hsplit.at[pl.ds(0, chips - 1)], send_sems.at[3])
        done(rs.at[pl.ds(0, chips - 1)], send_sems.at[4])
        done(tall.at[pl.ds(0, chips - 1)], send_sems.at[1])
        done(rg_all.at[pl.ds(0, chips - 1)], send_sems.at[5])
    if pair > 1:
        done(pn.at[0], send_sems.at[6])
        done(pgsend, send_sems.at[7])
        done(psend, send_sems.at[8])


def finish(a_ref, b_ref, c_ref, a_out, b_out, c_out, sems):
    copies = [
        pltpu.make_async_copy(src, dst, sems.at[i])
        for i, (src, dst) in enumerate(((a_ref, a_out), (b_ref, b_out), (c_ref, c_out)))
    ]
    for copy in copies:
        copy.start()
    for copy in copies:
        copy.wait()


def body(query_hidden, projection, page_embed, page_counts, positive, hard_negs, loss_weight):
    q_here, qlen, hidden = query_hidden.shape
    pages_here, slice_len, dim = page_embed.shape
    groups = lax.axis_size("grp")
    members = lax.axis_size("dev")
    n = groups * members
    rows = q_here * qlen
    q_total = n * q_here
    pair = 2 if groups % 2 == 0 else 1
    chips = n // pair
    zs = groups // pair
    both = pair * pages_here
    nb = math.gcd(chips, max(1, 256 // rows))
    n_chunks = chips // nb
    cq = nb * rows
    hb = hidden // n
    hb_pad = -(-hb // 128) * 128
    nhn = hard_negs.shape[1]
    vmem = pl.BlockSpec(memory_space=pltpu.VMEM)
    smem = pl.BlockSpec(memory_space=pltpu.SMEM)
    hbm = pl.BlockSpec(memory_space=pltpu.HBM)
    losses, hgrad, pgrad, pagegrad = pl.pallas_call(
        functools.partial(kernel, groups, members, qlen, nhn, nb),
        out_shape=(
            jax.ShapeDtypeStruct((q_here,), F32),
            jax.ShapeDtypeStruct((rows, hidden), BF16),
            jax.ShapeDtypeStruct((hb, dim), F32),
            jax.ShapeDtypeStruct((pages_here, slice_len, dim), BF16),
        ),
        in_specs=[hbm] * 8,
        out_specs=(smem, vmem, vmem, vmem),
        scratch_shapes=[
            pltpu.VMEM((rows, dim), BF16),
            pltpu.VMEM((chips, rows, dim), BF16),
            pltpu.VMEM((pair, pages_here, slice_len, dim), BF16),
            pltpu.VMEM((pages_here, slice_len, 1), F32),
            pltpu.VMEM((dim, both * slice_len), BF16),
            pltpu.VMEM((n_chunks, both, slice_len, cq), F32),
            pltpu.VMEM((n_chunks, both, cq), F32),
            pltpu.VMEM((n_chunks * both, cq), BF16),
            pltpu.VMEM((chips, n_chunks * both, cq), BF16),
            pltpu.VMEM((zs, n_chunks, both, cq), F32),
            pltpu.VMEM((zs, both, q_total), F32),
            pltpu.VMEM((n_chunks, cq, q_total), BF16),
            pltpu.VMEM((n_chunks, q_total, cq), BF16),
            pltpu.VMEM((chips, rows, pair * hb_pad), BF16),
            pltpu.VMEM((chips, rows, pair * hb_pad), BF16),
            pltpu.VMEM((pair, hb_pad, chips * rows), BF16),
            pltpu.VMEM((dim, hidden), BF16),
            pltpu.VMEM((n_chunks, both, slice_len, cq), BF16),
            pltpu.VMEM((chips, rows, dim), BF16),
            pltpu.VMEM((chips, rows, dim), BF16),
            pltpu.VMEM((rows, dim), BF16),
            pltpu.VMEM((chips, rows, dim), BF16),
            pltpu.VMEM((pages_here, slice_len, dim), BF16),
            pltpu.VMEM((pages_here, slice_len, dim), BF16),
            pltpu.VMEM((hb_pad, dim), F32),
            pltpu.VMEM((hb_pad, dim), F32),
            pltpu.SemaphoreType.DMA((9,)),
            pltpu.SemaphoreType.DMA((9,)),
            pltpu.SemaphoreType.DMA((n_chunks,)),
            pltpu.VMEM((rows, hidden), BF16),
            pltpu.VMEM((hidden, dim), BF16),
            pltpu.VMEM(page_embed.shape, BF16),
            pltpu.SMEM(page_counts.shape, jnp.int32),
            pltpu.VMEM((1, page_counts.shape[0]), jnp.int32),
            pltpu.VMEM((1, q_total), jnp.int32),
            pltpu.VMEM((nhn, q_total), jnp.int32),
            pltpu.VMEM((1, q_total), F32),
            pltpu.SemaphoreType.DMA((8,)),
        ],
        compiler_params=pltpu.CompilerParams(collective_id=0, has_side_effects=True),
    )(
        query_hidden.reshape(rows, hidden),
        projection,
        page_embed,
        page_counts,
        page_counts.reshape(1, -1),
        positive.reshape(1, q_total),
        hard_negs.T,
        loss_weight.reshape(1, q_total),
    )
    hgrad, pgrad, pagegrad = pl.pallas_call(
        finish,
        out_shape=(
            jax.ShapeDtypeStruct((q_here, qlen, hidden), BF16),
            jax.ShapeDtypeStruct((hb, dim), F32),
            jax.ShapeDtypeStruct((pages_here, slice_len, dim), BF16),
        ),
        in_specs=[vmem] * 3,
        out_specs=(hbm, hbm, hbm),
        scratch_shapes=[pltpu.SemaphoreType.DMA((3,))],
    )(hgrad.reshape(q_here, qlen, hidden), pgrad, pagegrad)
    return losses, hgrad, pgrad, pagegrad


def solution(mesh):
    in_specs = (P(("grp", "dev"), None, None), P(), P("grp", "dev", None), P(), P(), P(), P())
    out_specs = (
        P(("grp", "dev")),
        P(("grp", "dev"), None, None),
        P(("grp", "dev"), None),
        P("grp", "dev", None),
    )
    return jax.shard_map(body, mesh=mesh, in_specs=in_specs, out_specs=out_specs, check_vma=False)
```

```python
import functools
import math

import jax
import jax.numpy as jnp
from jax import lax
from jax.experimental import pallas as pl
from jax.experimental.pallas import tpu as pltpu
from jax.sharding import PartitionSpec as P

SOFTMAX_HEAT = 0.02
EPSILON = 1e-06
MESH = pl.DeviceIdType.MESH
NT = (((1,), (1,)), ((), ()))
F32 = jnp.float32
BF16 = jnp.bfloat16


def split3(x):
    a = x.astype(BF16)
    r = x - a.astype(F32)
    b = r.astype(BF16)
    c = (r - b.astype(F32)).astype(BF16)
    return a, b, c


def dot3(x, ind):
    a, b, c = split3(x)
    return (
        jnp.dot(c, ind, preferred_element_type=F32)
        + jnp.dot(b, ind, preferred_element_type=F32)
        + jnp.dot(a, ind, preferred_element_type=F32)
    )


def kernel(
    groups, members, qlen, nhn, nb,
    hid_in, proj_in, page_in, counts_in, crow_in, pos_in, neg_in, lw_in,
    loss_ref, hgrad_ref, pgrad_ref, pagegrad_ref,
    qsend, qall, pn, pscale, pnt, ebuf, tot, tx, tall, totz, sgbuf, ind_down, ind_up, hsplit, hall, hallt, projt,
    wbuf, qg, rs, rg, rg_all, pgsend, pgrecv, psend, precv,
    send_sems, recv_sems, q_sems,
    hid_ref, proj_ref, page_ref, counts_ref, crow_ref, pos_ref, neg_ref, lw_ref, load_sems,
):
    loads = [
        pltpu.make_async_copy(src, dst, load_sems.at[i])
        for i, (src, dst) in enumerate(
            (
                (hid_in, hid_ref), (proj_in, proj_ref), (page_in, page_ref), (counts_in, counts_ref),
                (crow_in, crow_ref), (pos_in, pos_ref), (neg_in, neg_ref), (lw_in, lw_ref),
            )
        )
    ]
    n = groups * members
    pair = pn.shape[0]
    chips = n // pair
    zs = groups // pair
    rows, hidden = hid_ref.shape
    pages_here, slice_len, dim = page_ref.shape
    both = pair * pages_here
    n_chunks = chips // nb
    cq = nb * rows
    q_here = rows // qlen
    q_total = n * q_here
    hb = hidden // n
    hb_pad = hallt.shape[1]
    gi = lax.axis_index("grp")
    mi = lax.axis_index("dev")
    me = gi * members + mi
    core = lax.rem(gi, pair)
    zi = lax.div(gi, pair)
    chip = zi * members + mi
    my_chunk = lax.div(chip, nb)
    partner = (gi + 1 - 2 * core, mi)

    def place(dst):
        return (lax.div(dst, members) * pair + core, lax.rem(dst, members))

    barrier = pltpu.get_barrier_semaphore()

    def greet(k, carry):
        where = place(lax.rem(chip + k, chips))
        pl.semaphore_signal(barrier, inc=1, device_id=where, device_id_type=MESH)
        return carry

    lax.fori_loop(1, chips, greet, 0)
    if pair > 1:
        pl.semaphore_signal(barrier, inc=1, device_id=partner, device_id_type=MESH)

    for load in loads:
        load.start()

    def done(ref, sem):
        pltpu.make_async_copy(ref, ref, sem).wait()

    def to_plane(src, dst, send_sem, recv_sem):
        def send(k, carry):
            where = place(lax.rem(chip + k, chips))
            pltpu.make_async_remote_copy(
                src, dst, send_sem, recv_sem, device_id=where, device_id_type=MESH
            ).start()
            return carry

        lax.fori_loop(1, chips, send, 0)

    def to_partner(src, dst, i):
        pltpu.make_async_remote_copy(
            src, dst, send_sems.at[i], recv_sems.at[i], device_id=partner, device_id_type=MESH
        ).start()

    loads[0].wait()
    loads[1].wait()
    query_raw = jnp.dot(hid_ref[...], proj_ref[...], preferred_element_type=F32)
    query_scale = lax.rsqrt(jnp.sum(query_raw * query_raw, axis=-1, keepdims=True) + EPSILON)
    query_unit = query_raw * query_scale
    qsend[...] = query_unit.astype(BF16)

    pl.semaphore_wait(barrier, chips - 1 + pair - 1)

    pltpu.make_async_copy(qsend, qall.at[chip], q_sems.at[my_chunk]).start()
    to_plane(qsend, qall.at[chip], send_sems.at[0], q_sems.at[my_chunk])

    loads[2].wait()
    for p in range(pages_here):
        praw = page_ref[p].astype(F32)
        ps = lax.rsqrt(jnp.sum(praw * praw, axis=-1, keepdims=True) + EPSILON)
        pscale[p] = ps
        pn[core, p] = (praw * ps).astype(BF16)
    if pair > 1:
        to_partner(pn.at[core], pn.at[core], 6)

    for j in range(chips):
        zj, mj = divmod(j, members)
        for h in range(pair):
            d = (zj * pair + h) * members + mj
            hsplit[j, :, h * hb_pad : h * hb_pad + hb] = hid_ref[:, d * hb : (d + 1) * hb]
            if hb_pad > hb:
                hsplit[j, :, h * hb_pad + hb : (h + 1) * hb_pad] = jnp.zeros((rows, hb_pad - hb), BF16)
    pltpu.make_async_copy(hsplit.at[chip], hall.at[chip], recv_sems.at[3]).start()

    def send_h(k, carry):
        dst = lax.rem(chip + k, chips)
        pltpu.make_async_remote_copy(
            hsplit.at[dst], hall.at[chip], send_sems.at[3], recv_sems.at[3],
            device_id=place(dst), device_id_type=MESH,
        ).start()
        return carry

    cut_a, cut_b = 1 + (chips - 1) // 3, 1 + 2 * (chips - 1) // 3
    lax.fori_loop(1, cut_a, send_h, 0)

    projt[...] = jnp.transpose(proj_ref[...])

    q_row = lax.broadcasted_iota(jnp.int32, (1, q_total), 1)
    q_col = lax.broadcasted_iota(jnp.int32, (q_total, 1), 0)

    def first_token(q):
        dev = lax.div(q, q_here)
        grp = lax.div(dev, members)
        at = (lax.div(grp, pair) * members + lax.rem(dev, members)) * rows + lax.rem(q, q_here) * qlen
        return jnp.where(lax.rem(grp, pair) == core, at, -qlen)

    row_start = first_token(q_row)
    col_start = first_token(q_col)

    def indicators(c, carry):
        r = lax.broadcasted_iota(jnp.int32, (cq, q_total), 0) + c * cq
        ind_down[c] = jnp.where((r >= row_start) & (r < row_start + qlen), 1.0, 0.0).astype(BF16)
        r = lax.broadcasted_iota(jnp.int32, (q_total, cq), 1) + c * cq
        ind_up[c] = jnp.where((r >= col_start) & (r < col_start + qlen), 1.0, 0.0).astype(BF16)
        return carry

    lax.fori_loop(0, n_chunks, indicators, 0)

    for load in loads[3:]:
        load.wait()
    token = lax.broadcasted_iota(jnp.int32, (slice_len, 1), 0) + mi * slice_len
    biases = []
    for p in range(both):
        count = counts_ref[zi * both + p]
        biases.append(jnp.where(token < count, 0.0, -1e30).astype(F32))

    page_total = groups * pages_here
    pos_row = pos_ref[...].astype(F32)
    neg_rows = [neg_ref[j : j + 1, :].astype(F32) for j in range(nhn)]
    lw_row = lw_ref[...]
    eye = lax.broadcasted_iota(jnp.int32, (page_total, page_total), 0) == lax.broadcasted_iota(
        jnp.int32, (page_total, page_total), 1
    )
    count_col = jnp.sum(jnp.where(eye, crow_ref[...].astype(F32), 0.0), axis=1, keepdims=True)
    log_count = (SOFTMAX_HEAT * qlen) * jnp.log(count_col)
    page_id = lax.broadcasted_iota(jnp.int32, (page_total, q_total), 0).astype(F32)
    pos_hot = jnp.where(page_id == pos_row, 1.0, 0.0)
    neg_hots = [jnp.where(page_id == row, 1.0, 0.0) for row in neg_rows]

    if pair > 1:
        done(pn.at[1 - core], recv_sems.at[6])

    def forward(i, carry):
        c = lax.rem(my_chunk + i, n_chunks)
        done(qall.at[pl.ds(0, nb)], q_sems.at[c])
        qc = qall[pl.ds(c * nb, nb)].reshape(cq, dim)
        parts = []
        for p in range(both):
            s = lax.dot_general(pn[p // pages_here, p % pages_here], qc, NT, preferred_element_type=F32)
            e = jnp.exp2(s * (math.log2(math.e) / SOFTMAX_HEAT) + biases[p])
            ebuf[c, p] = e
            parts.append(jnp.sum(e, axis=0, keepdims=True))
        tot[c] = jnp.concatenate(parts, axis=0)
        return carry

    lax.fori_loop(0, n_chunks, forward, 0)

    tx[...] = tot[...].reshape(n_chunks * both, cq).astype(BF16)
    pltpu.make_async_copy(tx, tall.at[chip], recv_sems.at[1]).start()
    to_plane(tx, tall.at[chip], send_sems.at[1], recv_sems.at[1])
    lax.fori_loop(cut_a, cut_b, send_h, 0)

    pnt[...] = jnp.transpose(pn[...].reshape(both * slice_len, dim))

    done(tall, recv_sems.at[1])

    for z in range(zs):

        def add_slices(m, acc):
            return acc + tall[z * members + m].astype(F32)

        if members <= 4:
            total = tall[z * members].astype(F32)
            for m in range(1, members):
                total = add_slices(m, total)
        else:
            total = lax.fori_loop(0, members, add_slices, jnp.zeros((n_chunks * both, cq), F32))
        totz[z] = total.reshape(n_chunks, both, cq)

    def compress(c, acc):
        return acc + dot3(jnp.log(totz[:, c].reshape(zs * both, cq)), ind_down[c])

    acc = jnp.zeros((page_total, q_total), F32)
    if n_chunks <= 4:
        for c in range(n_chunks):
            acc = compress(c, acc)
    else:
        acc = lax.fori_loop(0, n_chunks, compress, acc)
    scores = SOFTMAX_HEAT * acc - log_count

    log_total = jnp.log(jnp.sum(jnp.exp(scores), axis=0, keepdims=True))
    pos_score = jnp.sum(scores * pos_hot, axis=0, keepdims=True)
    soft = jnp.zeros((1, q_total), F32)
    push = jnp.zeros((page_total, q_total), F32)
    for j in range(nhn):
        margin = jnp.sum(scores * neg_hots[j], axis=0, keepdims=True) - pos_score
        small = jnp.exp(-jnp.abs(margin))
        soft = soft + jnp.maximum(margin, 0.0) + jnp.log1p(small)
        sig = jnp.where(margin >= 0, 1.0, small) / (1.0 + small)
        push = push + sig * (neg_hots[j] - pos_hot)
    losses = log_total - pos_score + soft / nhn
    grads = lw_row * (jnp.exp(scores - log_total) - pos_hot + push / nhn)
    for z in range(zs):
        sgbuf[z] = grads[z * both : (z + 1) * both, :]
    score_grad = sgbuf[zi]
    grad3 = split3(score_grad)

    def backward(i, carry):
        c = lax.rem(my_chunk + 1 + i, n_chunks)
        ind = ind_up[c]
        wide = (
            jnp.dot(grad3[2], ind, preferred_element_type=F32)
            + jnp.dot(grad3[1], ind, preferred_element_type=F32)
            + jnp.dot(grad3[0], ind, preferred_element_type=F32)
        )
        factor = wide / totz[zi, c]
        for p in range(both):
            wbuf[c, p] = (ebuf[c, p] * factor[p : p + 1, :]).astype(BF16)
        w = wbuf[c].reshape(both * slice_len, cq)
        gt = jnp.dot(pnt[...], w, preferred_element_type=F32)
        qg[pl.ds(c * nb, nb)] = jnp.transpose(gt).astype(BF16).reshape(nb, rows, dim)

        def send(k, carry2):
            dst = c * nb + k

            @pl.when(dst != chip)
            def _():
                pltpu.make_async_remote_copy(
                    qg.at[dst], rs.at[chip], send_sems.at[4], recv_sems.at[4],
                    device_id=place(dst), device_id_type=MESH,
                ).start()

            return carry2

        lax.fori_loop(0, nb, send, 0)
        return carry

    lax.fori_loop(0, n_chunks, backward, 0)
    pltpu.make_async_copy(qg.at[chip], rs.at[chip], recv_sems.at[4]).start()
    lax.fori_loop(cut_b, chips, send_h, 0)

    lane = lax.broadcasted_iota(jnp.int32, (1, q_total), 1)
    own = lax.broadcasted_iota(jnp.int32, (1, q_here), 1)
    mine = jnp.zeros((1, q_here), F32)
    for i in range(q_here):
        one = jnp.sum(jnp.where(lane == me * q_here + i, losses, 0.0), axis=1, keepdims=True)
        mine = jnp.where(own == i, one, mine)
    loss_ref[...] = mine

    def page_grad(half, p):
        def page_step(c, acc):
            qc = qall[pl.ds(c * nb, nb)].reshape(cq, dim)
            return acc + jnp.dot(wbuf[c, half * pages_here + p], qc, preferred_element_type=F32)

        acc = jnp.zeros((slice_len, dim), F32)
        if n_chunks <= 4:
            for c in range(n_chunks):
                acc = page_step(c, acc)
            return acc
        return lax.fori_loop(0, n_chunks, page_step, acc)

    if pair > 1:
        for p in range(pages_here):
            pgsend[p] = page_grad(1 - core, p).astype(BF16)
        to_partner(pgsend, pgrecv, 7)

    done(rs, recv_sems.at[4])
    sum_step = 8 if chips % 8 == 0 else 1

    def add(i, acc):
        return acc + jnp.sum(rs[pl.ds(i * sum_step, sum_step)].astype(F32), axis=0)

    query_grad = lax.fori_loop(0, chips // sum_step, add, jnp.zeros((rows, dim), F32))
    along = jnp.sum(query_unit * query_grad, axis=-1, keepdims=True)
    raw_grad = ((query_grad - query_unit * along) * query_scale).astype(BF16)
    rg[...] = raw_grad

    pltpu.make_async_copy(rg, rg_all.at[chip], recv_sems.at[5]).start()
    to_plane(rg, rg_all.at[chip], send_sems.at[5], recv_sems.at[5])

    own_grads = [page_grad(core, p) for p in range(pages_here)]
    if pair > 1:
        done(pgrecv, recv_sems.at[7])
    for p in range(pages_here):
        pg = own_grads[p]
        if pair > 1:
            pg = pg + pgrecv[p].astype(F32)
        ps = pscale[p]
        pu = page_ref[p].astype(F32) * ps
        back = jnp.sum(pu * pg, axis=-1, keepdims=True)
        pagegrad_ref[p] = ((pg - pu * back) * ps).astype(BF16)

    hgrad_ref[...] = jnp.dot(raw_grad, projt[...], preferred_element_type=F32).astype(BF16)

    done(hall, recv_sems.at[3])
    for h in range(pair):
        hallt[h] = jnp.transpose(hall[:, :, h * hb_pad : (h + 1) * hb_pad].reshape(chips * rows, hb_pad))

    done(rg_all, recv_sems.at[5])
    rga = rg_all[...].reshape(chips * rows, dim)
    if pair > 1:
        psend[...] = jnp.dot(hallt[1 - core], rga, preferred_element_type=F32)
        to_partner(psend, precv, 8)
    pgrad = jnp.dot(hallt[core], rga, preferred_element_type=F32)
    if pair > 1:
        done(precv, recv_sems.at[8])
        pgrad = pgrad + precv[...]
    pgrad_ref[...] = pgrad[:hb]
    if chips > 1:
        done(qall.at[pl.ds(0, chips - 1)], send_sems.at[0])
        done(hsplit.at[pl.ds(0, chips - 1)], send_sems.at[3])
        done(rs.at[pl.ds(0, chips - 1)], send_sems.at[4])
        done(tall.at[pl.ds(0, chips - 1)], send_sems.at[1])
        done(rg_all.at[pl.ds(0, chips - 1)], send_sems.at[5])
    if pair > 1:
        done(pn.at[0], send_sems.at[6])
        done(pgsend, send_sems.at[7])
        done(psend, send_sems.at[8])


def finish(a_ref, b_ref, c_ref, d_ref, a_out, b_out, c_out, d_out, sems):
    copies = [
        pltpu.make_async_copy(src, dst, sems.at[i])
        for i, (src, dst) in enumerate(((d_ref, d_out), (b_ref, b_out), (a_ref, a_out), (c_ref, c_out)))
    ]
    for copy in copies:
        copy.start()
    for copy in copies:
        copy.wait()


def body(query_hidden, projection, page_embed, page_counts, positive, hard_negs, loss_weight):
    q_here, qlen, hidden = query_hidden.shape
    pages_here, slice_len, dim = page_embed.shape
    groups = lax.axis_size("grp")
    members = lax.axis_size("dev")
    n = groups * members
    rows = q_here * qlen
    q_total = n * q_here
    pair = 2 if groups % 2 == 0 else 1
    chips = n // pair
    zs = groups // pair
    both = pair * pages_here
    nb = math.gcd(chips, max(1, 256 // rows))
    n_chunks = chips // nb
    cq = nb * rows
    hb = hidden // n
    hb_pad = -(-hb // 128) * 128
    nhn = hard_negs.shape[1]
    vmem = pl.BlockSpec(memory_space=pltpu.VMEM)
    smem = pl.BlockSpec(memory_space=pltpu.SMEM)
    hbm = pl.BlockSpec(memory_space=pltpu.HBM)
    losses, hgrad, pgrad, pagegrad = pl.pallas_call(
        functools.partial(kernel, groups, members, qlen, nhn, nb),
        out_shape=(
            jax.ShapeDtypeStruct((1, q_here), F32),
            jax.ShapeDtypeStruct((rows, hidden), BF16),
            jax.ShapeDtypeStruct((hb, dim), F32),
            jax.ShapeDtypeStruct((pages_here, slice_len, dim), BF16),
        ),
        in_specs=[hbm] * 8,
        out_specs=(vmem, vmem, vmem, vmem),
        scratch_shapes=[
            pltpu.VMEM((rows, dim), BF16),
            pltpu.VMEM((chips, rows, dim), BF16),
            pltpu.VMEM((pair, pages_here, slice_len, dim), BF16),
            pltpu.VMEM((pages_here, slice_len, 1), F32),
            pltpu.VMEM((dim, both * slice_len), BF16),
            pltpu.VMEM((n_chunks, both, slice_len, cq), F32),
            pltpu.VMEM((n_chunks, both, cq), F32),
            pltpu.VMEM((n_chunks * both, cq), BF16),
            pltpu.VMEM((chips, n_chunks * both, cq), BF16),
            pltpu.VMEM((zs, n_chunks, both, cq), F32),
            pltpu.VMEM((zs, both, q_total), F32),
            pltpu.VMEM((n_chunks, cq, q_total), BF16),
            pltpu.VMEM((n_chunks, q_total, cq), BF16),
            pltpu.VMEM((chips, rows, pair * hb_pad), BF16),
            pltpu.VMEM((chips, rows, pair * hb_pad), BF16),
            pltpu.VMEM((pair, hb_pad, chips * rows), BF16),
            pltpu.VMEM((dim, hidden), BF16),
            pltpu.VMEM((n_chunks, both, slice_len, cq), BF16),
            pltpu.VMEM((chips, rows, dim), BF16),
            pltpu.VMEM((chips, rows, dim), BF16),
            pltpu.VMEM((rows, dim), BF16),
            pltpu.VMEM((chips, rows, dim), BF16),
            pltpu.VMEM((pages_here, slice_len, dim), BF16),
            pltpu.VMEM((pages_here, slice_len, dim), BF16),
            pltpu.VMEM((hb_pad, dim), F32),
            pltpu.VMEM((hb_pad, dim), F32),
            pltpu.SemaphoreType.DMA((9,)),
            pltpu.SemaphoreType.DMA((9,)),
            pltpu.SemaphoreType.DMA((n_chunks,)),
            pltpu.VMEM((rows, hidden), BF16),
            pltpu.VMEM((hidden, dim), BF16),
            pltpu.VMEM(page_embed.shape, BF16),
            pltpu.SMEM(page_counts.shape, jnp.int32),
            pltpu.VMEM((1, page_counts.shape[0]), jnp.int32),
            pltpu.VMEM((1, q_total), jnp.int32),
            pltpu.VMEM((nhn, q_total), jnp.int32),
            pltpu.VMEM((1, q_total), F32),
            pltpu.SemaphoreType.DMA((8,)),
        ],
        compiler_params=pltpu.CompilerParams(collective_id=0, has_side_effects=True),
    )(
        query_hidden.reshape(rows, hidden),
        projection,
        page_embed,
        page_counts,
        page_counts.reshape(1, -1),
        positive.reshape(1, q_total),
        hard_negs.T,
        loss_weight.reshape(1, q_total),
    )
    hgrad, pgrad, pagegrad, losses = pl.pallas_call(
        finish,
        out_shape=(
            jax.ShapeDtypeStruct((q_here, qlen, hidden), BF16),
            jax.ShapeDtypeStruct((hb, dim), F32),
            jax.ShapeDtypeStruct((pages_here, slice_len, dim), BF16),
            jax.ShapeDtypeStruct((1, q_here), F32),
        ),
        in_specs=[vmem, vmem, vmem, vmem],
        out_specs=(hbm, hbm, hbm, hbm),
        scratch_shapes=[pltpu.SemaphoreType.DMA((4,))],
    )(hgrad.reshape(q_here, qlen, hidden), pgrad, pagegrad, losses)
    return losses.reshape(q_here), hgrad, pgrad, pagegrad


def solution(mesh):
    in_specs = (P(("grp", "dev"), None, None), P(), P("grp", "dev", None), P(), P(), P(), P())
    out_specs = (
        P(("grp", "dev")),
        P(("grp", "dev"), None, None),
        P(("grp", "dev"), None),
        P("grp", "dev", None),
    )
    return jax.shard_map(body, mesh=mesh, in_specs=in_specs, out_specs=out_specs, check_vma=False)
```

```python
import functools
import math

import jax
import jax.numpy as jnp
from jax import lax
from jax.experimental import pallas as pl
from jax.experimental.pallas import tpu as pltpu
from jax.sharding import PartitionSpec as P

SOFTMAX_HEAT = 0.02
EPSILON = 1e-06
MESH = pl.DeviceIdType.MESH
NT = (((1,), (1,)), ((), ()))
F32 = jnp.float32
BF16 = jnp.bfloat16


def split3(x):
    a = x.astype(BF16)
    r = x - a.astype(F32)
    b = r.astype(BF16)
    c = (r - b.astype(F32)).astype(BF16)
    return a, b, c


def dot3(x, ind):
    a, b, c = split3(x)
    return (
        jnp.dot(c, ind, preferred_element_type=F32)
        + jnp.dot(b, ind, preferred_element_type=F32)
        + jnp.dot(a, ind, preferred_element_type=F32)
    )


def kernel(
    groups, members, qlen, nhn, nb,
    hid_in, proj_in, page_in, counts_in, crow_in, pos_in, neg_in, lw_in,
    loss_out, hgrad_out, pgrad_ref, pagegrad_out,
    qsend, qall, pn, pscale, pnt, ebuf, tot, tx, tall, totz, sgbuf, ind_down, ind_up, hsplit, hall, hallt, projt,
    wbuf, qg, rs, rg, rg_all, pgsend, pgrecv, psend, precv,
    send_sems, recv_sems, q_sems,
    hid_ref, proj_ref, page_ref, counts_ref, crow_ref, pos_ref, neg_ref, lw_ref, load_sems,
    loss_ref, hgrad_ref, pagegrad_ref, out_sems,
):
    loads = [
        pltpu.make_async_copy(src, dst, load_sems.at[i])
        for i, (src, dst) in enumerate(
            (
                (hid_in, hid_ref), (proj_in, proj_ref), (page_in, page_ref), (counts_in, counts_ref),
                (crow_in, crow_ref), (pos_in, pos_ref), (neg_in, neg_ref), (lw_in, lw_ref),
            )
        )
    ]
    n = groups * members
    pair = pn.shape[0]
    chips = n // pair
    zs = groups // pair
    rows, hidden = hid_ref.shape
    pages_here, slice_len, dim = page_ref.shape
    both = pair * pages_here
    n_chunks = chips // nb
    cq = nb * rows
    q_here = rows // qlen
    q_total = n * q_here
    hb = hidden // n
    hb_pad = hallt.shape[1]
    gi = lax.axis_index("grp")
    mi = lax.axis_index("dev")
    me = gi * members + mi
    core = lax.rem(gi, pair)
    zi = lax.div(gi, pair)
    chip = zi * members + mi
    my_chunk = lax.div(chip, nb)
    partner = (gi + 1 - 2 * core, mi)

    def place(dst):
        return (lax.div(dst, members) * pair + core, lax.rem(dst, members))

    barrier = pltpu.get_barrier_semaphore()

    def greet(k, carry):
        where = place(lax.rem(chip + k, chips))
        pl.semaphore_signal(barrier, inc=1, device_id=where, device_id_type=MESH)
        return carry

    lax.fori_loop(1, chips, greet, 0)
    if pair > 1:
        pl.semaphore_signal(barrier, inc=1, device_id=partner, device_id_type=MESH)

    for load in loads:
        load.start()

    def done(ref, sem):
        pltpu.make_async_copy(ref, ref, sem).wait()

    def to_plane(src, dst, send_sem, recv_sem):
        def send(k, carry):
            where = place(lax.rem(chip + k, chips))
            pltpu.make_async_remote_copy(
                src, dst, send_sem, recv_sem, device_id=where, device_id_type=MESH
            ).start()
            return carry

        lax.fori_loop(1, chips, send, 0)

    def to_partner(src, dst, i):
        pltpu.make_async_remote_copy(
            src, dst, send_sems.at[i], recv_sems.at[i], device_id=partner, device_id_type=MESH
        ).start()

    loads[0].wait()
    loads[1].wait()
    query_raw = jnp.dot(hid_ref[...], proj_ref[...], preferred_element_type=F32)
    query_scale = lax.rsqrt(jnp.sum(query_raw * query_raw, axis=-1, keepdims=True) + EPSILON)
    query_unit = query_raw * query_scale
    qsend[...] = query_unit.astype(BF16)

    pl.semaphore_wait(barrier, chips - 1 + pair - 1)

    pltpu.make_async_copy(qsend, qall.at[chip], q_sems.at[my_chunk]).start()
    to_plane(qsend, qall.at[chip], send_sems.at[0], q_sems.at[my_chunk])

    loads[2].wait()
    for p in range(pages_here):
        praw = page_ref[p].astype(F32)
        ps = lax.rsqrt(jnp.sum(praw * praw, axis=-1, keepdims=True) + EPSILON)
        pscale[p] = ps
        pn[core, p] = (praw * ps).astype(BF16)
    if pair > 1:
        to_partner(pn.at[core], pn.at[core], 6)

    for j in range(chips):
        zj, mj = divmod(j, members)
        for h in range(pair):
            d = (zj * pair + h) * members + mj
            hsplit[j, :, h * hb_pad : h * hb_pad + hb] = hid_ref[:, d * hb : (d + 1) * hb]
            if hb_pad > hb:
                hsplit[j, :, h * hb_pad + hb : (h + 1) * hb_pad] = jnp.zeros((rows, hb_pad - hb), BF16)
    pltpu.make_async_copy(hsplit.at[chip], hall.at[chip], recv_sems.at[3]).start()

    def send_h(k, carry):
        dst = lax.rem(chip + k, chips)
        pltpu.make_async_remote_copy(
            hsplit.at[dst], hall.at[chip], send_sems.at[3], recv_sems.at[3],
            device_id=place(dst), device_id_type=MESH,
        ).start()
        return carry

    cut_a, cut_b = 1 + (chips - 1) // 3, 1 + 2 * (chips - 1) // 3
    lax.fori_loop(1, cut_a, send_h, 0)

    projt[...] = jnp.transpose(proj_ref[...])

    q_row = lax.broadcasted_iota(jnp.int32, (1, q_total), 1)
    q_col = lax.broadcasted_iota(jnp.int32, (q_total, 1), 0)

    def first_token(q):
        dev = lax.div(q, q_here)
        grp = lax.div(dev, members)
        at = (lax.div(grp, pair) * members + lax.rem(dev, members)) * rows + lax.rem(q, q_here) * qlen
        return jnp.where(lax.rem(grp, pair) == core, at, -qlen)

    row_start = first_token(q_row)
    col_start = first_token(q_col)

    def indicators(c, carry):
        r = lax.broadcasted_iota(jnp.int32, (cq, q_total), 0) + c * cq
        ind_down[c] = jnp.where((r >= row_start) & (r < row_start + qlen), 1.0, 0.0).astype(BF16)
        r = lax.broadcasted_iota(jnp.int32, (q_total, cq), 1) + c * cq
        ind_up[c] = jnp.where((r >= col_start) & (r < col_start + qlen), 1.0, 0.0).astype(BF16)
        return carry

    lax.fori_loop(0, n_chunks, indicators, 0)

    for load in loads[3:]:
        load.wait()
    token = lax.broadcasted_iota(jnp.int32, (slice_len, 1), 0) + mi * slice_len
    biases = []
    for p in range(both):
        count = counts_ref[zi * both + p]
        biases.append(jnp.where(token < count, 0.0, -1e30).astype(F32))

    page_total = groups * pages_here
    pos_row = pos_ref[...].astype(F32)
    neg_rows = [neg_ref[j : j + 1, :].astype(F32) for j in range(nhn)]
    lw_row = lw_ref[...]
    eye = lax.broadcasted_iota(jnp.int32, (page_total, page_total), 0) == lax.broadcasted_iota(
        jnp.int32, (page_total, page_total), 1
    )
    count_col = jnp.sum(jnp.where(eye, crow_ref[...].astype(F32), 0.0), axis=1, keepdims=True)
    log_count = (SOFTMAX_HEAT * qlen) * jnp.log(count_col)
    page_id = lax.broadcasted_iota(jnp.int32, (page_total, q_total), 0).astype(F32)
    pos_hot = jnp.where(page_id == pos_row, 1.0, 0.0)
    neg_hots = [jnp.where(page_id == row, 1.0, 0.0) for row in neg_rows]

    if pair > 1:
        done(pn.at[1 - core], recv_sems.at[6])

    def forward(i, carry):
        c = lax.rem(my_chunk + i, n_chunks)
        done(qall.at[pl.ds(0, nb)], q_sems.at[c])
        qc = qall[pl.ds(c * nb, nb)].reshape(cq, dim)
        parts = []
        for p in range(both):
            s = lax.dot_general(pn[p // pages_here, p % pages_here], qc, NT, preferred_element_type=F32)
            e = jnp.exp2(s * (math.log2(math.e) / SOFTMAX_HEAT) + biases[p])
            ebuf[c, p] = e
            parts.append(jnp.sum(e, axis=0, keepdims=True))
        tot[c] = jnp.concatenate(parts, axis=0)
        return carry

    lax.fori_loop(0, n_chunks, forward, 0)

    tx[...] = tot[...].reshape(n_chunks * both, cq).astype(BF16)
    pltpu.make_async_copy(tx, tall.at[chip], recv_sems.at[1]).start()
    to_plane(tx, tall.at[chip], send_sems.at[1], recv_sems.at[1])
    lax.fori_loop(cut_a, cut_b, send_h, 0)

    pnt[...] = jnp.transpose(pn[...].reshape(both * slice_len, dim))

    done(tall, recv_sems.at[1])

    for z in range(zs):

        def add_slices(m, acc):
            return acc + tall[z * members + m].astype(F32)

        if members <= 4:
            total = tall[z * members].astype(F32)
            for m in range(1, members):
                total = add_slices(m, total)
        else:
            total = lax.fori_loop(0, members, add_slices, jnp.zeros((n_chunks * both, cq), F32))
        totz[z] = total.reshape(n_chunks, both, cq)

    def compress(c, acc):
        return acc + dot3(jnp.log(totz[:, c].reshape(zs * both, cq)), ind_down[c])

    acc = jnp.zeros((page_total, q_total), F32)
    if n_chunks <= 4:
        for c in range(n_chunks):
            acc = compress(c, acc)
    else:
        acc = lax.fori_loop(0, n_chunks, compress, acc)
    scores = SOFTMAX_HEAT * acc - log_count

    log_total = jnp.log(jnp.sum(jnp.exp(scores), axis=0, keepdims=True))
    pos_score = jnp.sum(scores * pos_hot, axis=0, keepdims=True)
    soft = jnp.zeros((1, q_total), F32)
    push = jnp.zeros((page_total, q_total), F32)
    for j in range(nhn):
        margin = jnp.sum(scores * neg_hots[j], axis=0, keepdims=True) - pos_score
        small = jnp.exp(-jnp.abs(margin))
        soft = soft + jnp.maximum(margin, 0.0) + jnp.log1p(small)
        sig = jnp.where(margin >= 0, 1.0, small) / (1.0 + small)
        push = push + sig * (neg_hots[j] - pos_hot)
    losses = log_total - pos_score + soft / nhn
    grads = lw_row * (jnp.exp(scores - log_total) - pos_hot + push / nhn)
    for z in range(zs):
        sgbuf[z] = grads[z * both : (z + 1) * both, :]
    score_grad = sgbuf[zi]
    grad3 = split3(score_grad)

    def backward(i, carry):
        c = lax.rem(my_chunk + 1 + i, n_chunks)
        ind = ind_up[c]
        wide = (
            jnp.dot(grad3[2], ind, preferred_element_type=F32)
            + jnp.dot(grad3[1], ind, preferred_element_type=F32)
            + jnp.dot(grad3[0], ind, preferred_element_type=F32)
        )
        factor = wide / totz[zi, c]
        for p in range(both):
            wbuf[c, p] = (ebuf[c, p] * factor[p : p + 1, :]).astype(BF16)
        w = wbuf[c].reshape(both * slice_len, cq)
        gt = jnp.dot(pnt[...], w, preferred_element_type=F32)
        qg[pl.ds(c * nb, nb)] = jnp.transpose(gt).astype(BF16).reshape(nb, rows, dim)

        def send(k, carry2):
            dst = c * nb + k

            @pl.when(dst != chip)
            def _():
                pltpu.make_async_remote_copy(
                    qg.at[dst], rs.at[chip], send_sems.at[4], recv_sems.at[4],
                    device_id=place(dst), device_id_type=MESH,
                ).start()

            return carry2

        lax.fori_loop(0, nb, send, 0)
        return carry

    lax.fori_loop(0, n_chunks, backward, 0)
    pltpu.make_async_copy(qg.at[chip], rs.at[chip], recv_sems.at[4]).start()
    lax.fori_loop(cut_b, chips, send_h, 0)

    lane = lax.broadcasted_iota(jnp.int32, (1, q_total), 1)
    own = lax.broadcasted_iota(jnp.int32, (1, q_here), 1)
    mine = jnp.zeros((1, q_here), F32)
    for i in range(q_here):
        one = jnp.sum(jnp.where(lane == me * q_here + i, losses, 0.0), axis=1, keepdims=True)
        mine = jnp.where(own == i, one, mine)
    loss_ref[...] = mine
    store_loss = pltpu.make_async_copy(loss_ref, loss_out, out_sems.at[0])
    store_loss.start()

    def page_grad(half, p):
        def page_step(c, acc):
            qc = qall[pl.ds(c * nb, nb)].reshape(cq, dim)
            return acc + jnp.dot(wbuf[c, half * pages_here + p], qc, preferred_element_type=F32)

        acc = jnp.zeros((slice_len, dim), F32)
        if n_chunks <= 4:
            for c in range(n_chunks):
                acc = page_step(c, acc)
            return acc
        return lax.fori_loop(0, n_chunks, page_step, acc)

    if pair > 1:
        for p in range(pages_here):
            pgsend[p] = page_grad(1 - core, p).astype(BF16)
        to_partner(pgsend, pgrecv, 7)

    done(rs, recv_sems.at[4])
    sum_step = 8 if chips % 8 == 0 else 1

    def add(i, acc):
        return acc + jnp.sum(rs[pl.ds(i * sum_step, sum_step)].astype(F32), axis=0)

    query_grad = lax.fori_loop(0, chips // sum_step, add, jnp.zeros((rows, dim), F32))
    along = jnp.sum(query_unit * query_grad, axis=-1, keepdims=True)
    raw_grad = ((query_grad - query_unit * along) * query_scale).astype(BF16)
    rg[...] = raw_grad

    pltpu.make_async_copy(rg, rg_all.at[chip], recv_sems.at[5]).start()
    to_plane(rg, rg_all.at[chip], send_sems.at[5], recv_sems.at[5])

    own_grads = [page_grad(core, p) for p in range(pages_here)]
    if pair > 1:
        done(pgrecv, recv_sems.at[7])
    for p in range(pages_here):
        pg = own_grads[p]
        if pair > 1:
            pg = pg + pgrecv[p].astype(F32)
        ps = pscale[p]
        pu = page_ref[p].astype(F32) * ps
        back = jnp.sum(pu * pg, axis=-1, keepdims=True)
        pagegrad_ref[p] = ((pg - pu * back) * ps).astype(BF16)
    store_pages = pltpu.make_async_copy(pagegrad_ref, pagegrad_out, out_sems.at[1])
    store_pages.start()

    hgrad_ref[...] = jnp.dot(raw_grad, projt[...], preferred_element_type=F32).astype(BF16)
    store_hidden = pltpu.make_async_copy(hgrad_ref, hgrad_out, out_sems.at[2])
    store_hidden.start()

    done(hall, recv_sems.at[3])
    for h in range(pair):
        hallt[h] = jnp.transpose(hall[:, :, h * hb_pad : (h + 1) * hb_pad].reshape(chips * rows, hb_pad))

    done(rg_all, recv_sems.at[5])
    rga = rg_all[...].reshape(chips * rows, dim)
    if pair > 1:
        psend[...] = jnp.dot(hallt[1 - core], rga, preferred_element_type=F32)
        to_partner(psend, precv, 8)
    pgrad = jnp.dot(hallt[core], rga, preferred_element_type=F32)
    if pair > 1:
        done(precv, recv_sems.at[8])
        pgrad = pgrad + precv[...]
    pgrad_ref[...] = pgrad[:hb]
    store_loss.wait()
    store_pages.wait()
    store_hidden.wait()
    if chips > 1:
        done(qall.at[pl.ds(0, chips - 1)], send_sems.at[0])
        done(hsplit.at[pl.ds(0, chips - 1)], send_sems.at[3])
        done(rs.at[pl.ds(0, chips - 1)], send_sems.at[4])
        done(tall.at[pl.ds(0, chips - 1)], send_sems.at[1])
        done(rg_all.at[pl.ds(0, chips - 1)], send_sems.at[5])
    if pair > 1:
        done(pn.at[0], send_sems.at[6])
        done(pgsend, send_sems.at[7])
        done(psend, send_sems.at[8])


def finish(a_in, b_in, c_in, d_in, a_out, b_out, c_out, d_out, a_buf, b_buf, c_buf, d_buf, in_sems, out_sems):
    moves = ((b_in, b_buf, b_out), (d_in, d_buf, d_out), (a_in, a_buf, a_out), (c_in, c_buf, c_out))
    loads = [pltpu.make_async_copy(src, buf, in_sems.at[i]) for i, (src, buf, _) in enumerate(moves)]
    stores = [pltpu.make_async_copy(buf, dst, out_sems.at[i]) for i, (_, buf, dst) in enumerate(moves)]
    for load in loads:
        load.start()
    for load, store in zip(loads, stores, strict=True):
        load.wait()
        store.start()
    for store in stores:
        store.wait()


def body(query_hidden, projection, page_embed, page_counts, positive, hard_negs, loss_weight):
    q_here, qlen, hidden = query_hidden.shape
    pages_here, slice_len, dim = page_embed.shape
    groups = lax.axis_size("grp")
    members = lax.axis_size("dev")
    n = groups * members
    rows = q_here * qlen
    q_total = n * q_here
    pair = 2 if groups % 2 == 0 else 1
    chips = n // pair
    zs = groups // pair
    both = pair * pages_here
    nb = math.gcd(chips, max(1, 256 // rows))
    n_chunks = chips // nb
    cq = nb * rows
    hb = hidden // n
    hb_pad = -(-hb // 128) * 128
    nhn = hard_negs.shape[1]
    vmem = pl.BlockSpec(memory_space=pltpu.VMEM)
    smem = pl.BlockSpec(memory_space=pltpu.SMEM)
    hbm = pl.BlockSpec(memory_space=pltpu.HBM)
    losses, hgrad, pgrad, pagegrad = pl.pallas_call(
        functools.partial(kernel, groups, members, qlen, nhn, nb),
        out_shape=(
            jax.ShapeDtypeStruct((1, q_here), F32),
            jax.ShapeDtypeStruct((rows, hidden), BF16),
            jax.ShapeDtypeStruct((hb, dim), F32),
            jax.ShapeDtypeStruct((pages_here, slice_len, dim), BF16),
        ),
        in_specs=[hbm] * 8,
        out_specs=(hbm, hbm, vmem, hbm),
        scratch_shapes=[
            pltpu.VMEM((rows, dim), BF16),
            pltpu.VMEM((chips, rows, dim), BF16),
            pltpu.VMEM((pair, pages_here, slice_len, dim), BF16),
            pltpu.VMEM((pages_here, slice_len, 1), F32),
            pltpu.VMEM((dim, both * slice_len), BF16),
            pltpu.VMEM((n_chunks, both, slice_len, cq), F32),
            pltpu.VMEM((n_chunks, both, cq), F32),
            pltpu.VMEM((n_chunks * both, cq), BF16),
            pltpu.VMEM((chips, n_chunks * both, cq), BF16),
            pltpu.VMEM((zs, n_chunks, both, cq), F32),
            pltpu.VMEM((zs, both, q_total), F32),
            pltpu.VMEM((n_chunks, cq, q_total), BF16),
            pltpu.VMEM((n_chunks, q_total, cq), BF16),
            pltpu.VMEM((chips, rows, pair * hb_pad), BF16),
            pltpu.VMEM((chips, rows, pair * hb_pad), BF16),
            pltpu.VMEM((pair, hb_pad, chips * rows), BF16),
            pltpu.VMEM((dim, hidden), BF16),
            pltpu.VMEM((n_chunks, both, slice_len, cq), BF16),
            pltpu.VMEM((chips, rows, dim), BF16),
            pltpu.VMEM((chips, rows, dim), BF16),
            pltpu.VMEM((rows, dim), BF16),
            pltpu.VMEM((chips, rows, dim), BF16),
            pltpu.VMEM((pages_here, slice_len, dim), BF16),
            pltpu.VMEM((pages_here, slice_len, dim), BF16),
            pltpu.VMEM((hb_pad, dim), F32),
            pltpu.VMEM((hb_pad, dim), F32),
            pltpu.SemaphoreType.DMA((9,)),
            pltpu.SemaphoreType.DMA((9,)),
            pltpu.SemaphoreType.DMA((n_chunks,)),
            pltpu.VMEM((rows, hidden), BF16),
            pltpu.VMEM((hidden, dim), BF16),
            pltpu.VMEM(page_embed.shape, BF16),
            pltpu.SMEM(page_counts.shape, jnp.int32),
            pltpu.VMEM((1, page_counts.shape[0]), jnp.int32),
            pltpu.VMEM((1, q_total), jnp.int32),
            pltpu.VMEM((nhn, q_total), jnp.int32),
            pltpu.VMEM((1, q_total), F32),
            pltpu.SemaphoreType.DMA((8,)),
            pltpu.VMEM((1, q_here), F32),
            pltpu.VMEM((rows, hidden), BF16),
            pltpu.VMEM(page_embed.shape, BF16),
            pltpu.SemaphoreType.DMA((3,)),
        ],
        compiler_params=pltpu.CompilerParams(collective_id=0, has_side_effects=True),
    )(
        query_hidden.reshape(rows, hidden),
        projection,
        page_embed,
        page_counts,
        page_counts.reshape(1, -1),
        positive.reshape(1, q_total),
        hard_negs.T,
        loss_weight.reshape(1, q_total),
    )
    hgrad, pgrad, pagegrad, losses = pl.pallas_call(
        finish,
        out_shape=(
            jax.ShapeDtypeStruct((q_here, qlen, hidden), BF16),
            jax.ShapeDtypeStruct((hb, dim), F32),
            jax.ShapeDtypeStruct((pages_here, slice_len, dim), BF16),
            jax.ShapeDtypeStruct((1, q_here), F32),
        ),
        in_specs=[hbm] * 4,
        out_specs=(hbm, hbm, hbm, hbm),
        scratch_shapes=[
            pltpu.VMEM((q_here, qlen, hidden), BF16),
            pltpu.VMEM((hb, dim), F32),
            pltpu.VMEM((pages_here, slice_len, dim), BF16),
            pltpu.VMEM((1, q_here), F32),
            pltpu.SemaphoreType.DMA((4,)),
            pltpu.SemaphoreType.DMA((4,)),
        ],
    )(hgrad.reshape(q_here, qlen, hidden), pgrad, pagegrad, losses)
    return losses.reshape(q_here), hgrad, pgrad, pagegrad


def solution(mesh):
    in_specs = (P(("grp", "dev"), None, None), P(), P("grp", "dev", None), P(), P(), P(), P())
    out_specs = (
        P(("grp", "dev")),
        P(("grp", "dev"), None, None),
        P(("grp", "dev"), None),
        P("grp", "dev", None),
    )
    return jax.shard_map(body, mesh=mesh, in_specs=in_specs, out_specs=out_specs, check_vma=False)
```
